32 devices in a mesh: row: 8 (over y, x, core), col: 4 (over z).
Axes of the slice: x: 2, y: 2, z: 4, core: 2. Of those that a mesh axis runs over, the one named last changes fastest.
Arguments:
- alignment: float32 [192, 16, 64], P('row', 'col'), may hold values from -6 to 6
- pair_state: float32 [192, 192, 128], P('row', 'col'), may hold values from -6 to 6
- pair_weights: float32 [8, 192, 192], P(None, 'row', 'col'), may hold values from 0 to 1, as said below
- align_gain: float32 [64], replicated, may hold values from 0.5 to 2
- value_weight: float32 [64, 256], replicated, may hold values from -0.75 to 0.75
- gate_weight: float32 [64, 256], replicated, may hold values from -0.75 to 0.75
- output_weight: float32 [256, 64], replicated, may hold values from -0.375 to 0.375
- outer_gain: float32 [64], replicated, may hold values from 0.5 to 2
- left_weight: float32 [64, 32], replicated, may hold values from -0.75 to 0.75
- right_weight: float32 [64, 32], replicated, may hold values from -0.75 to 0.75
- outer_weight: float32 [1024, 128], replicated, may hold values from -0.75 to 0.75
- outer_bias: float32 [128], replicated, may hold values from -3 to 3
Outputs:
- alignment_out: float32 [192, 16, 64], P('row', 'col')
- pair_out: float32 [192, 192, 128], P('row', 'col')
The draws below stay inside these ranges and needn't reach their ends.
Inputs may be any that keep to these rules, and one draw needn't show every extreme that they name: `pair_weights`: every entry is positive, and for each head and row token the weights over the 192 column tokens sum to one.
All inputs are finite; a program needn't handle non-finite values.
Results may differ from the reference program's by a relative error of at most 0.00011.
Values sent between devices are 32-bit elements; how exact they have to be, the bound alone decides.
A program may use at most 64 MiB of HBM per device.

```python
import math
import jax
import jax.numpy as jnp
from jax import lax

CM = 64
CZ = 128
HEADS = 8
HEAD_DIM = 32
OUTER = 32
ROWS_DEV = 24
TOKENS = 192
SEQS = 16


def draw_pair_weights(key, part):
    logit_key = jax.random.fold_in(jax.random.fold_in(key, 17), 0)
    logits = 3.0 * jax.random.normal(logit_key, (HEADS, TOKENS, TOKENS), jnp.float32)
    return jax.nn.softmax(logits, axis=-1)


def level_of(key, extent, shards, low, high):
    loudness, own = 1.0, jax.random.fold_in(key, 6)
    for position, parts in shards:
        heights = jnp.exp(jax.random.uniform(jax.random.fold_in(own, position), (parts,), jnp.float32, low / len(shards), high / len(shards)))
        loudness = loudness * jnp.repeat(heights, extent[position] // parts).reshape([-1 if axis == position else 1 for axis in range(len(extent))])
    return loudness


def gaussian(stream_key, shape, scale, reach, pieces=(), held_as=jnp.bfloat16):
    entries = jax.random.normal(stream_key, shape, jnp.float32) * scale
    if len(pieces) > 0:
        entries = level_of(stream_key, shape, pieces, -0.22, 0.18) * entries
    return jnp.clip(entries, min=-reach, max=reach).astype(held_as)


def setup_inputs(seed: int = 0) -> dict:
    arg_keys = jax.random.split(jax.random.key(seed), 13)
    return {
        "alignment": gaussian(arg_keys[0], (TOKENS, SEQS, CM), 1.0, 6.0, ((0, 8), (1, 4)), jnp.float32),
        "pair_state": gaussian(arg_keys[1], (TOKENS, TOKENS, CZ), 1.0, 6.0, ((0, 8), (1, 4)), jnp.float32),
        "pair_weights": draw_pair_weights(jax.random.fold_in(arg_keys[12], 71), 0),
        "align_gain": jnp.clip(jnp.exp(jax.random.uniform(arg_keys[3], (CM,), jnp.float32, math.log(0.5), math.log(2.0))), 0.5, 2.0),
        "value_weight": gaussian(arg_keys[4], (CM, HEADS * HEAD_DIM), CM ** -0.5, 0.75, (), jnp.float32),
        "gate_weight": gaussian(arg_keys[5], (CM, HEADS * HEAD_DIM), CM ** -0.5, 0.75, (), jnp.float32),
        "output_weight": gaussian(arg_keys[6], (HEADS * HEAD_DIM, CM), (HEADS * HEAD_DIM) ** -0.5, 0.375, (), jnp.float32),
        "outer_gain": jnp.clip(jnp.exp(jax.random.uniform(arg_keys[7], (CM,), jnp.float32, math.log(0.5), math.log(2.0))), 0.5, 2.0),
        "left_weight": gaussian(arg_keys[8], (CM, OUTER), CM ** -0.5, 0.75, (), jnp.float32),
        "right_weight": gaussian(arg_keys[9], (CM, OUTER), CM ** -0.5, 0.75, (), jnp.float32),
        "outer_weight": gaussian(arg_keys[10], (OUTER * OUTER, CZ), (max(OUTER * OUTER // 16, 1)) ** -0.5, 0.75, (), jnp.float32),
        "outer_bias": gaussian(arg_keys[11], (CZ,), 0.5, 3.0, (), jnp.float32),
    }


PRECISE = lax.Precision.HIGHEST

def normalize(features, channel_gain):
    channel_mean = lax.optimization_barrier(jnp.mean(features, axis=-1, keepdims=True))
    centered = features - channel_mean
    spread = lax.optimization_barrier(jnp.mean(centered * centered, axis=-1, keepdims=True))
    return centered * lax.rsqrt(spread + 1e-05) * channel_gain

def reference(alignment, pair_state, pair_weights, align_gain, value_weight, gate_weight, output_weight, outer_gain, left_weight, right_weight, outer_weight, outer_bias):
    head_count = pair_weights.shape[0]
    normed = normalize(alignment, align_gain)
    values = jnp.einsum('nsc,cd->nsd', normed, value_weight, precision=PRECISE)
    values = values.reshape(values.shape[0], values.shape[1], head_count, -1)
    averaged = jnp.einsum('hij,jshd->ishd', pair_weights, values, precision=PRECISE)
    gate_values = jax.nn.sigmoid(jnp.einsum('nsc,cd->nsd', normed, gate_weight, precision=PRECISE))
    gated_heads = gate_values * averaged.reshape(gate_values.shape)
    alignment_out = alignment + jnp.einsum('nsd,dc->nsc', gated_heads, output_weight, precision=PRECISE)
    normed_out = normalize(alignment_out, outer_gain)
    left_side = jnp.einsum('nsc,cd->nsd', normed_out, left_weight, precision=PRECISE)
    right_side = jnp.einsum('nsc,cd->nsd', normed_out, right_weight, precision=PRECISE)
    sequences = alignment.shape[1]
    left_blocks = left_side.reshape(-1, ROWS_DEV, sequences, left_side.shape[2])

    def outer_block(left_block):
        product = jnp.einsum('isc,jsd->ijcd', left_block, right_side, precision=PRECISE) / sequences
        flattened = product.reshape(-1, product.shape[2] * product.shape[3])
        projected = jnp.dot(flattened, outer_weight, precision=PRECISE, preferred_element_type=jnp.float32)
        return projected.reshape(left_block.shape[0], right_side.shape[0], -1)
    update = lax.map(outer_block, left_blocks).reshape(pair_state.shape)
    pair_out = pair_state + update + outer_bias
    return (alignment_out, pair_out)
```

```python
import functools

import jax
import jax.numpy as jnp
from jax import lax
from jax.experimental import pallas as pl
from jax.experimental.pallas import tpu as pltpu
from jax.sharding import PartitionSpec as P

MESH = pl.DeviceIdType.MESH
F32, BF16 = jnp.float32, jnp.bfloat16


def dot(a, b):
    return jnp.dot(a, b, preferred_element_type=F32)


def split(a):
    hi = a.astype(BF16)
    return hi, (a - hi.astype(F32)).astype(BF16)


def stack(a):
    hi = a.astype(BF16).astype(F32)
    return jnp.concatenate([hi, a - hi], axis=0).astype(BF16)


def fold_rows(a):
    half = a.shape[0] // 2
    return a[:half] + a[half:]


def dot3(a, bh, bl):
    return fold_rows(dot(stack(a), bh)) + dot(a.astype(BF16), bl)


def iotas(shape):
    return (
        lax.broadcasted_iota(jnp.int32, shape, 0),
        lax.broadcasted_iota(jnp.int32, shape, 1),
    )


def div(x, n):
    return x >> (n.bit_length() - 1) if n & (n - 1) == 0 else lax.div(x, jnp.int32(n))


def rem(x, n):
    return x & (n - 1) if n & (n - 1) == 0 else lax.rem(x, jnp.int32(n))


def block_diagonal(w, copies):
    rows, cols = w.shape
    wide = jnp.concatenate([w] * copies, axis=1)
    tall = jnp.concatenate([wide] * copies, axis=0)
    r, c = iotas(tall.shape)
    return jnp.where(div(r, rows) == div(c, cols), tall, 0.0)


def kernel(
    n_row, n_col, heads, fold, columns,
    x_ref, w_ref, ag_ref, v_ref, g_ref, o_ref, og_ref, lw_ref, rw_ref, ow_hbm,
    a_out, upd_out,
    xbuf, wbuf, lr, lbuf, rbuf, ow, wp, perm, lp, th, tl,
    bd_v, bd_g, bd_o, bd_lr,
    sx, rx, sw, rws, sl, rl, sr, rr, ow_sem,
):
    r, c = lax.axis_index("row"), lax.axis_index("col")
    rows, width = x_ref.shape
    channels = v_ref.shape[0]
    seqs = width // channels
    factor = lw_ref.shape[1]
    lanes = seqs * factor
    all_seqs = seqs * n_col
    per = columns // rows
    home = r // per
    slot = r % per
    is_home = home == c
    mine = (r, c)

    load_ow = pltpu.make_async_copy(ow_hbm, ow, ow_sem)
    load_ow.start()

    barrier = pltpu.get_barrier_semaphore()
    for k in range(1, n_row):
        pl.semaphore_signal(barrier, 1, device_id=((r + k) % n_row, c), device_id_type=MESH)
    for k in range(1, n_col):
        pl.semaphore_signal(barrier, 1, device_id=(r, (c + k) % n_col), device_id_type=MESH)
    for a in range(per):
        for k in range(n_col):
            src_r = c * per + a

            @pl.when(jnp.logical_and(src_r != r, k != c))
            def _():
                pl.semaphore_signal(barrier, 1, device_id=(src_r, jnp.int32(k)), device_id_type=MESH)

    @pl.when(is_home)
    def _():
        pl.semaphore_wait(barrier, n_row - 1 + n_col - 1)

    @pl.when(jnp.logical_not(is_home))
    def _():
        pl.semaphore_wait(barrier, n_row - 1 + n_col - 1 + n_row - 1)

    def remote(src, dst, send, recv, device):
        return pltpu.make_async_remote_copy(
            src_ref=src, dst_ref=dst, send_sem=send, recv_sem=recv,
            device_id=device, device_id_type=MESH,
        )

    sends = []
    for k in range(1, n_col):
        cp = remote(w_ref, wbuf.at[c], sw.at[k], rws.at[c], (r, (c + k) % n_col))
        cp.start()
        sends.append(cp)
    for k in range(1, n_row):
        cp = remote(x_ref, xbuf.at[r], sx.at[k], rx.at[r], ((r + k) % n_row, c))
        cp.start()
        sends.append(cp)

    xbuf[r] = x_ref[...]
    wbuf[c] = w_ref[...]
    part = v_ref.shape[1] // fold
    for a in range(fold):
        lo_l, hi_l = a * part, (a + 1) * part
        for ref, bd, w in (
            (v_ref, bd_v, v_ref[:, lo_l:hi_l]),
            (g_ref, bd_g, g_ref[:, lo_l:hi_l]),
            (o_ref, bd_o, o_ref[lo_l:hi_l, :]),
        ):
            h, l = split(block_diagonal(w, seqs))
            bd[a, 0] = h
            bd[a, 1] = l
    h, l = split(
        jnp.concatenate(
            [block_diagonal(lw_ref[...], seqs), block_diagonal(rw_ref[...], seqs)], axis=1
        )
    )
    bd_lr[0] = h
    bd_lr[1] = l
    pr, pc = iotas(perm.shape)
    perm[...] = jnp.where(
        pr == rem(pc, all_seqs) * factor + div(pc, all_seqs), 1.0, 0.0
    ).astype(BF16)

    mr, mc = iotas((width, width))
    mean_of = jnp.where(div(mr, channels) == div(mc, channels), 1.0 / channels, 0.0).astype(BF16)

    def normalize(x, gain):
        cen = x - fold_rows(dot(stack(x), mean_of))
        var = fold_rows(dot(stack(cen * cen), mean_of))
        return cen * lax.rsqrt(var + 1e-05) * gain

    gain = jnp.concatenate([ag_ref[...]] * seqs, axis=1)
    out_gain = jnp.concatenate([og_ref[...]] * seqs, axis=1)
    own = normalize(x_ref[...], gain)
    gates = [
        1.0 / (1.0 + jnp.exp(-dot3(own, bd_g[a, 0], bd_g[a, 1]))) for a in range(fold)
    ]

    load_ow.wait()
    z = ow.shape[1]
    for d in range(factor):
        h, l = split(ow[pl.ds(d, factor, stride=factor), :])
        wp[:, d * z : (d + 1) * z] = jnp.concatenate([h, h, l], axis=0)

    for k in range(1, n_row):
        s = (r + k) % n_row
        remote(x_ref, xbuf.at[s], sx.at[k], rx.at[s], (s, c)).wait_recv()
    nh, nl = split(normalize(xbuf[...].reshape(n_row * rows, width), gain))
    kpad = w_ref.shape[1] - fold * columns

    def spread(n):
        parts = []
        for cc in range(n_col):
            blk = n[cc * columns : (cc + 1) * columns]
            for a in range(fold):
                parts.append(
                    jnp.concatenate(
                        [blk if b == a else jnp.zeros_like(blk) for b in range(fold)], axis=1
                    )
                )
            if kpad:
                parts.append(jnp.zeros((kpad, fold * width), BF16))
        return jnp.concatenate(parts, axis=0)

    sh, sl_ = spread(nh), spread(nl)
    for k in range(1, n_col):
        s = (c + k) % n_col
        remote(w_ref, wbuf.at[s], sw.at[k], rws.at[s], (r, s)).wait_recv()
    wide = jnp.concatenate([wbuf[cc] for cc in range(n_col)], axis=1)
    mixed = dot3(wide, sh, sl_)
    hpart = heads // fold
    head_dim = part // hpart
    res = x_ref[...]
    for a in range(fold):
        full = dot3(mixed[:, a * width : (a + 1) * width], bd_v[a, 0], bd_v[a, 1])
        _, lane = iotas((rows, seqs * part))
        head_of = rem(div(lane, head_dim), hpart)
        avg = jnp.zeros((rows, seqs * part), F32)
        for hh in range(hpart):
            avg = jnp.where(head_of == hh, full[hh * rows : (hh + 1) * rows], avg)
        res = res + dot3(gates[a] * avg, bd_o[a, 0], bd_o[a, 1])
    a_out[...] = res
    both = dot3(normalize(res, out_gain), bd_lr[0], bd_lr[1])
    lr[0] = both[:, :lanes]
    lr[1] = both[:, lanes:]

    for k in range(1, n_col):
        cp = remote(lr.at[0], lbuf.at[c], sl.at[k], rl.at[c], (r, (c + k) % n_col))
        cp.start()
        sends.append(cp)
    for k in range(1, n_row):
        cp = remote(lr.at[1], rbuf.at[slot, c], sr.at[k], rr.at[slot, c], ((r + k) % n_row, home))
        cp.start()
        sends.append(cp)
    to_home = remote(lr.at[1], rbuf.at[slot, c], sr.at[0], rr.at[slot, c], (r, home))

    @pl.when(jnp.logical_not(is_home))
    def _():
        to_home.start()

    @pl.when(is_home)
    def _():
        rbuf[slot, c] = both[:, lanes:]

    lbuf[c] = both[:, :lanes]
    for k in range(1, n_col):
        s = (c + k) % n_col
        remote(lr.at[0], lbuf.at[s], sl.at[k], rl.at[s], (r, s)).wait_recv()
    for cc in range(n_col):
        blk = lbuf[cc]
        hi = blk.astype(BF16).astype(F32)
        lo = blk - hi
        for s in range(seqs):
            cut = slice(s * factor, (s + 1) * factor)
            pieces = [hi[:, cut], lo[:, cut], hi[:, cut], jnp.zeros((rows, lp.shape[1] - 3 * factor), F32)]
            lp[pl.ds(cc * seqs + s, rows, stride=all_seqs), :] = jnp.concatenate(pieces, axis=1)

    pairs = th.shape[0]
    block = pairs * 2

    def make_t(first):
        left = lp[pl.ds(pl.multiple_of(first * all_seqs, 8), block * all_seqs), :][
            :, : 3 * factor
        ].astype(BF16)
        for d in range(0, factor, 2):
            t = dot(left, wp[:, d * z : (d + 2) * z])
            for e in range(2):
                h, l = split(t[:, e * z : (e + 1) * z])
                h = h.reshape(pairs, 2, all_seqs, z)
                l = l.reshape(pairs, 2, all_seqs, z)
                at = slice((d + e) * all_seqs, (d + e + 1) * all_seqs)
                for q in range(2):
                    th[:, at, q * z : (q + 1) * z] = h[:, q]
                    tl[:, at, q * z : (q + 1) * z] = l[:, q]

    make_t(0)

    for a in range(per):
        for cc in range(n_col):

            @pl.when(jnp.logical_not(jnp.logical_and(c * per + a == r, cc == c)))
            def _():
                remote(
                    lr.at[1], rbuf.at[a, cc], sr.at[0], rr.at[a, cc], (c * per + a, jnp.int32(cc))
                ).wait_recv()

    right = jnp.concatenate(
        [jnp.concatenate([rbuf[a, cc] for cc in range(n_col)], axis=1) for a in range(per)], axis=0
    ) * (1.0 / all_seqs)
    right2 = dot(stack(right), perm[...]).astype(BF16)
    right1 = right2[:columns]

    def finish(first):
        for q in range(pairs):
            u = fold_rows(dot(right2, th[q])) + dot(right1, tl[q])
            upd_out[first + 2 * q] = u[:, :z]
            upd_out[first + 2 * q + 1] = u[:, z:]

    finish(0)
    if rows > block:

        def step(i, _):
            make_t(i * block)
            finish(i * block)
            return 0

        lax.fori_loop(1, rows // block, step, 0)

    for cp in sends:
        cp.wait_send()

    @pl.when(jnp.logical_not(is_home))
    def _():
        to_home.wait_send()


def on_device(
    n_row, n_col,
    alignment, pair_state, pair_weights, align_gain, value_weight, gate_weight,
    output_weight, outer_gain, left_weight, right_weight, outer_weight, outer_bias,
):
    heads = pair_weights.shape[0]
    rows, seqs, channels = alignment.shape
    columns = pair_state.shape[1]
    z = pair_state.shape[2]
    factor = left_weight.shape[1]
    hidden = value_weight.shape[1]
    all_seqs = seqs * n_col
    width = seqs * channels
    fold = max(1, 128 // columns)
    while heads % fold:
        fold -= 1
    wide = -(-fold * columns // 128) * 128
    x2 = alignment.reshape(rows, width)
    w2 = pair_weights.reshape(fold, heads // fold * rows, columns)
    w2 = jnp.concatenate([w2[a] for a in range(fold)], axis=1)
    w2 = jnp.pad(w2, ((0, 0), (0, wide - fold * columns)))
    block = 2
    for b in range(2, rows + 1, 2):
        if rows % b == 0 and b * all_seqs <= 384:
            block = b
    per = columns // rows
    part = hidden // fold
    vmem = pl.BlockSpec(memory_space=pltpu.VMEM)
    dma = pltpu.SemaphoreType.DMA
    a_out, update = pl.pallas_call(
        functools.partial(kernel, n_row, n_col, heads, fold, columns),
        name="msa_block",
        out_shape=(
            jax.ShapeDtypeStruct((rows, width), F32),
            jax.ShapeDtypeStruct((rows, columns, z), F32),
        ),
        in_specs=[vmem] * 9 + [pl.BlockSpec(memory_space=pl.ANY)],
        out_specs=(vmem, vmem),
        scratch_shapes=[
            pltpu.VMEM((n_row, rows, width), F32),
            pltpu.VMEM((n_col, w2.shape[0], wide), F32),
            pltpu.VMEM((2, rows, seqs * factor), F32),
            pltpu.VMEM((n_col, rows, seqs * factor), F32),
            pltpu.VMEM((per, n_col, rows, seqs * factor), F32),
            pltpu.VMEM(outer_weight.shape, F32),
            pltpu.VMEM((3 * factor, factor * z), BF16),
            pltpu.VMEM((all_seqs * factor, all_seqs * factor), BF16),
            pltpu.VMEM((rows * all_seqs, 128), F32),
            pltpu.VMEM((block // 2, all_seqs * factor, 2 * z), BF16),
            pltpu.VMEM((block // 2, all_seqs * factor, 2 * z), BF16),
            pltpu.VMEM((fold, 2, width, seqs * part), BF16),
            pltpu.VMEM((fold, 2, width, seqs * part), BF16),
            pltpu.VMEM((fold, 2, seqs * part, width), BF16),
            pltpu.VMEM((2, width, 2 * seqs * factor), BF16),
            dma((n_row,)),
            dma((n_row,)),
            dma((n_col,)),
            dma((n_col,)),
            dma((n_col,)),
            dma((n_col,)),
            dma((n_row,)),
            dma((per, n_col)),
            dma(()),
        ],
        compiler_params=pltpu.CompilerParams(collective_id=0, has_side_effects=True),
    )(
        x2, w2, align_gain.reshape(1, -1), value_weight, gate_weight, output_weight,
        outer_gain.reshape(1, -1), left_weight, right_weight, outer_weight,
    )
    pair_out = pair_state + update + outer_bias
    return (a_out.reshape(alignment.shape), pair_out)


def solution(mesh):
    n_row, n_col = mesh.shape["row"], mesh.shape["col"]
    return jax.shard_map(
        functools.partial(on_device, n_row, n_col),
        mesh=mesh,
        in_specs=(
            P("row", "col", None),
            P("row", "col", None),
            P(None, "row", "col"),
        )
        + (P(),) * 9,
        out_specs=(P("row", "col", None), P("row", "col", None)),
        check_vma=False,
    )
```

```python
import functools

import jax
import jax.numpy as jnp
from jax import lax
from jax.experimental import pallas as pl
from jax.experimental.pallas import tpu as pltpu
from jax.sharding import PartitionSpec as P

MESH = pl.DeviceIdType.MESH
F32, BF16 = jnp.float32, jnp.bfloat16


def dot(a, b):
    return jnp.dot(a, b, preferred_element_type=F32)


def split(a):
    hi = a.astype(BF16)
    return hi, (a - hi.astype(F32)).astype(BF16)


def stack(a):
    hi = a.astype(BF16).astype(F32)
    return jnp.concatenate([hi, a - hi], axis=0).astype(BF16)


def fold_rows(a):
    half = a.shape[0] // 2
    return a[:half] + a[half:]


def dot3(a, bh, bl):
    return fold_rows(dot(stack(a), bh)) + dot(a.astype(BF16), bl)


def iotas(shape):
    return (
        lax.broadcasted_iota(jnp.int32, shape, 0),
        lax.broadcasted_iota(jnp.int32, shape, 1),
    )


def div(x, n):
    return x >> (n.bit_length() - 1) if n & (n - 1) == 0 else lax.div(x, jnp.int32(n))


def rem(x, n):
    return x & (n - 1) if n & (n - 1) == 0 else lax.rem(x, jnp.int32(n))


def block_diagonal(w, copies):
    rows, cols = w.shape
    wide = jnp.concatenate([w] * copies, axis=1)
    tall = jnp.concatenate([wide] * copies, axis=0)
    r, c = iotas(tall.shape)
    return jnp.where(div(r, rows) == div(c, cols), tall, 0.0)


def kernel(n_row, n_col, heads, fold, columns, *refs):
    inputs, (a_out, upd_out), local = refs[:11], refs[11:13], refs[13:24]
    x_in, w_in, ag_ref, v_ref, g_ref, ot_ref, og_ref, lwt_ref, rwt_ref, bias_ref, ow = local
    (
    x_ref, w_ref, xbuf, wbuf, lr, lbuf, rbuf, wp, perm, lp, th, tl,
    bd_v, bd_g, bd_o, bd_lr,
    sx, rx, sw, rws, sl, rl, sr, rr, in_sem,
    ) = refs[24:]
    r, c = lax.axis_index("row"), lax.axis_index("col")
    rows, width = x_ref.shape
    channels = v_ref.shape[0]
    seqs = width // channels
    factor = lwt_ref.shape[0]
    lanes = seqs * factor
    all_seqs = seqs * n_col
    per = columns // rows
    home = r // per
    slot = r % per
    is_home = home == c
    mine = (r, c)

    loads = [pltpu.make_async_copy(a, b, in_sem.at[k]) for k, (a, b) in enumerate(zip(inputs, local))]
    for load in loads:
        load.start()

    barrier = pltpu.get_barrier_semaphore()
    for k in range(1, n_row):
        pl.semaphore_signal(barrier, 1, device_id=((r + k) % n_row, c), device_id_type=MESH)
    for k in range(1, n_col):
        pl.semaphore_signal(barrier, 1, device_id=(r, (c + k) % n_col), device_id_type=MESH)
    for a in range(per):
        for k in range(n_col):
            src_r = c * per + a

            @pl.when(jnp.logical_and(src_r != r, k != c))
            def _():
                pl.semaphore_signal(barrier, 1, device_id=(src_r, jnp.int32(k)), device_id_type=MESH)

    loads[0].wait()
    loads[1].wait()
    x_ref[...] = jnp.concatenate([x_in[:, s, :] for s in range(seqs)], axis=1)
    half = w_ref.shape[0]
    packed = [w_in[a * half : (a + 1) * half, :] for a in range(fold)]
    kpad = w_ref.shape[1] - fold * columns
    if kpad:
        packed.append(jnp.zeros((half, kpad), F32))
    w_ref[...] = jnp.concatenate(packed, axis=1)

    @pl.when(is_home)
    def _():
        pl.semaphore_wait(barrier, n_row - 1 + n_col - 1)

    @pl.when(jnp.logical_not(is_home))
    def _():
        pl.semaphore_wait(barrier, n_row - 1 + n_col - 1 + n_row - 1)

    def remote(src, dst, send, recv, device):
        return pltpu.make_async_remote_copy(
            src_ref=src, dst_ref=dst, send_sem=send, recv_sem=recv,
            device_id=device, device_id_type=MESH,
        )

    sends = []
    for k in range(1, n_col):
        cp = remote(w_ref, wbuf.at[c], sw.at[k], rws.at[c], (r, (c + k) % n_col))
        cp.start()
        sends.append(cp)
    for k in range(1, n_row):
        cp = remote(x_ref, xbuf.at[r], sx.at[k], rx.at[r], ((r + k) % n_row, c))
        cp.start()
        sends.append(cp)

    xbuf[r] = x_ref[...]
    wbuf[c] = w_ref[...]
    for load in loads[2:]:
        load.wait()
    part = v_ref.shape[1] // fold
    o_w = ot_ref[...].T
    for a in range(fold):
        lo_l, hi_l = a * part, (a + 1) * part
        for ref, bd, w in (
            (v_ref, bd_v, v_ref[:, lo_l:hi_l]),
            (g_ref, bd_g, g_ref[:, lo_l:hi_l]),
            (ot_ref, bd_o, o_w[lo_l:hi_l, :]),
        ):
            h, l = split(block_diagonal(w, seqs))
            bd[a, 0] = h
            bd[a, 1] = l
    h, l = split(
        jnp.concatenate(
            [block_diagonal(ref[...].T, seqs) for ref in (lwt_ref, rwt_ref)], axis=1
        )
    )
    bd_lr[0] = h
    bd_lr[1] = l
    pr, pc = iotas(perm.shape)
    perm[...] = jnp.where(
        pr == rem(pc, all_seqs) * factor + div(pc, all_seqs), 1.0, 0.0
    ).astype(BF16)

    mr, mc = iotas((width, width))
    mean_of = jnp.where(div(mr, channels) == div(mc, channels), 1.0 / channels, 0.0).astype(BF16)

    def normalize(x, gain):
        cen = x - fold_rows(dot(stack(x), mean_of))
        var = fold_rows(dot(stack(cen * cen), mean_of))
        return cen * lax.rsqrt(var + 1e-05) * gain

    gain = jnp.concatenate([ag_ref[...]] * seqs, axis=1)
    out_gain = jnp.concatenate([og_ref[...]] * seqs, axis=1)
    own = normalize(x_ref[...], gain)
    gates = [
        1.0 / (1.0 + jnp.exp(-dot3(own, bd_g[a, 0], bd_g[a, 1]))) for a in range(fold)
    ]

    z = ow.shape[1]
    for d in range(factor):
        h, l = split(ow[pl.ds(d, factor, stride=factor), :])
        wp[:, d * z : (d + 1) * z] = jnp.concatenate([h, h, l], axis=0)

    for k in range(1, n_row):
        s = (r + k) % n_row
        remote(x_ref, xbuf.at[s], sx.at[k], rx.at[s], (s, c)).wait_recv()
    nh, nl = split(normalize(xbuf[...].reshape(n_row * rows, width), gain))

    def spread(n):
        parts = []
        for cc in range(n_col):
            blk = n[cc * columns : (cc + 1) * columns]
            for a in range(fold):
                parts.append(
                    jnp.concatenate(
                        [blk if b == a else jnp.zeros_like(blk) for b in range(fold)], axis=1
                    )
                )
            if kpad:
                parts.append(jnp.zeros((kpad, fold * width), BF16))
        return jnp.concatenate(parts, axis=0)

    sh, sl_ = spread(nh), spread(nl)
    for k in range(1, n_col):
        s = (c + k) % n_col
        remote(w_ref, wbuf.at[s], sw.at[k], rws.at[s], (r, s)).wait_recv()
    wide = jnp.concatenate([wbuf[cc] for cc in range(n_col)], axis=1)
    mixed = dot3(wide, sh, sl_)
    hpart = heads // fold
    head_dim = part // hpart
    res = x_ref[...]
    for a in range(fold):
        full = dot3(mixed[:, a * width : (a + 1) * width], bd_v[a, 0], bd_v[a, 1])
        _, lane = iotas((rows, seqs * part))
        head_of = rem(div(lane, head_dim), hpart)
        avg = jnp.zeros((rows, seqs * part), F32)
        for hh in range(hpart):
            avg = jnp.where(head_of == hh, full[hh * rows : (hh + 1) * rows], avg)
        res = res + dot3(gates[a] * avg, bd_o[a, 0], bd_o[a, 1])
    a_out[...] = res
    both = dot3(normalize(res, out_gain), bd_lr[0], bd_lr[1])
    lr[0] = both[:, :lanes]
    lr[1] = both[:, lanes:]

    for k in range(1, n_col):
        cp = remote(lr.at[0], lbuf.at[c], sl.at[k], rl.at[c], (r, (c + k) % n_col))
        cp.start()
        sends.append(cp)
    for k in range(1, n_row):
        cp = remote(lr.at[1], rbuf.at[slot, c], sr.at[k], rr.at[slot, c], ((r + k) % n_row, home))
        cp.start()
        sends.append(cp)
    to_home = remote(lr.at[1], rbuf.at[slot, c], sr.at[0], rr.at[slot, c], (r, home))

    @pl.when(jnp.logical_not(is_home))
    def _():
        to_home.start()

    @pl.when(is_home)
    def _():
        rbuf[slot, c] = both[:, lanes:]

    lbuf[c] = both[:, :lanes]
    for k in range(1, n_col):
        s = (c + k) % n_col
        remote(lr.at[0], lbuf.at[s], sl.at[k], rl.at[s], (r, s)).wait_recv()
    for cc in range(n_col):
        blk = lbuf[cc]
        hi = blk.astype(BF16).astype(F32)
        lo = blk - hi
        for s in range(seqs):
            cut = slice(s * factor, (s + 1) * factor)
            pieces = [hi[:, cut], lo[:, cut], hi[:, cut], jnp.zeros((rows, lp.shape[1] - 3 * factor), F32)]
            lp[pl.ds(cc * seqs + s, rows, stride=all_seqs), :] = jnp.concatenate(pieces, axis=1)

    pairs = th.shape[0]
    block = pairs * 2

    def make_t(first):
        left = lp[pl.ds(pl.multiple_of(first * all_seqs, 8), block * all_seqs), :][
            :, : 3 * factor
        ].astype(BF16)
        for d in range(0, factor, 2):
            t = dot(left, wp[:, d * z : (d + 2) * z])
            for e in range(2):
                h, l = split(t[:, e * z : (e + 1) * z])
                h = h.reshape(pairs, 2, all_seqs, z)
                l = l.reshape(pairs, 2, all_seqs, z)
                at = slice((d + e) * all_seqs, (d + e + 1) * all_seqs)
                for q in range(2):
                    th[:, at, q * z : (q + 1) * z] = h[:, q]
                    tl[:, at, q * z : (q + 1) * z] = l[:, q]

    make_t(0)

    for a in range(per):
        for cc in range(n_col):

            @pl.when(jnp.logical_not(jnp.logical_and(c * per + a == r, cc == c)))
            def _():
                remote(
                    lr.at[1], rbuf.at[a, cc], sr.at[0], rr.at[a, cc], (c * per + a, jnp.int32(cc))
                ).wait_recv()

    right = jnp.concatenate(
        [jnp.concatenate([rbuf[a, cc] for cc in range(n_col)], axis=1) for a in range(per)], axis=0
    ) * (1.0 / all_seqs)
    right2 = dot(stack(right), perm[...]).astype(BF16)
    right1 = right2[:columns]

    bias2 = jnp.concatenate([bias_ref[...]] * 2, axis=1)

    def finish(first):
        for q in range(pairs):
            u = fold_rows(dot(right2, th[q])) + dot(right1, tl[q]) + bias2
            upd_out[first + 2 * q] = u[:, :z]
            upd_out[first + 2 * q + 1] = u[:, z:]

    finish(0)
    if rows > block:

        def step(i, _):
            make_t(i * block)
            finish(i * block)
            return 0

        lax.fori_loop(1, rows // block, step, 0)

    for cp in sends:
        cp.wait_send()

    @pl.when(jnp.logical_not(is_home))
    def _():
        to_home.wait_send()


def on_device(
    n_row, n_col,
    alignment, pair_state, pair_weights, align_gain, value_weight, gate_weight,
    output_weight, outer_gain, left_weight, right_weight, outer_weight, outer_bias,
):
    heads = pair_weights.shape[0]
    rows, seqs, channels = alignment.shape
    columns = pair_state.shape[1]
    z = pair_state.shape[2]
    factor = left_weight.shape[1]
    hidden = value_weight.shape[1]
    all_seqs = seqs * n_col
    width = seqs * channels
    fold = max(1, 128 // columns)
    while heads % fold:
        fold -= 1
    wide = -(-fold * columns // 128) * 128
    half = heads // fold * rows
    block = 2
    for b in range(2, rows + 1, 2):
        if rows % b == 0 and b * all_seqs <= 384:
            block = b
    per = columns // rows
    part = hidden // fold
    vmem = pl.BlockSpec(memory_space=pltpu.VMEM)
    dma = pltpu.SemaphoreType.DMA
    operands = (
        alignment, pair_weights.reshape(heads * rows, columns), align_gain.reshape(1, -1),
        value_weight, gate_weight, output_weight.T, outer_gain.reshape(1, -1),
        left_weight.T, right_weight.T, outer_bias.reshape(1, -1), outer_weight,
    )
    a_out, update = pl.pallas_call(
        functools.partial(kernel, n_row, n_col, heads, fold, columns),
        name="msa_block",
        out_shape=(
            jax.ShapeDtypeStruct((rows, width), F32),
            pltpu.VMEM((rows, columns, z), F32),
        ),
        in_specs=[pl.BlockSpec(memory_space=pltpu.HBM)] * len(operands),
        out_specs=(vmem, vmem),
        scratch_shapes=[pltpu.VMEM(operand.shape, F32) for operand in operands]
        + [
            pltpu.VMEM((rows, width), F32),
            pltpu.VMEM((half, wide), F32),
            pltpu.VMEM((n_row, rows, width), F32),
            pltpu.VMEM((n_col, half, wide), F32),
            pltpu.VMEM((2, rows, seqs * factor), F32),
            pltpu.VMEM((n_col, rows, seqs * factor), F32),
            pltpu.VMEM((per, n_col, rows, seqs * factor), F32),
            pltpu.VMEM((3 * factor, factor * z), BF16),
            pltpu.VMEM((all_seqs * factor, all_seqs * factor), BF16),
            pltpu.VMEM((rows * all_seqs, 128), F32),
            pltpu.VMEM((block // 2, all_seqs * factor, 2 * z), BF16),
            pltpu.VMEM((block // 2, all_seqs * factor, 2 * z), BF16),
            pltpu.VMEM((fold, 2, width, seqs * part), BF16),
            pltpu.VMEM((fold, 2, width, seqs * part), BF16),
            pltpu.VMEM((fold, 2, seqs * part, width), BF16),
            pltpu.VMEM((2, width, 2 * seqs * factor), BF16),
            dma((n_row,)),
            dma((n_row,)),
            dma((n_col,)),
            dma((n_col,)),
            dma((n_col,)),
            dma((n_col,)),
            dma((n_row,)),
            dma((per, n_col)),
            dma((len(operands),)),
        ],
        compiler_params=pltpu.CompilerParams(collective_id=0, has_side_effects=True, vmem_limit_bytes=67043328 - 4 * rows * columns * z - (64 << 10)),
    )(*operands)
    pair_out = pair_state + update
    return (a_out.reshape(alignment.shape), pair_out)


def solution(mesh):
    n_row, n_col = mesh.shape["row"], mesh.shape["col"]
    return jax.shard_map(
        functools.partial(on_device, n_row, n_col),
        mesh=mesh,
        in_specs=(
            P("row", "col", None),
            P("row", "col", None),
            P(None, "row", "col"),
        )
        + (P(),) * 9,
        out_specs=(P("row", "col", None), P("row", "col", None)),
        check_vma=False,
    )
```

```python
import functools

import jax
import jax.numpy as jnp
from jax import lax
from jax.experimental import pallas as pl
from jax.experimental.pallas import tpu as pltpu
from jax.sharding import PartitionSpec as P

MESH = pl.DeviceIdType.MESH
F32, BF16 = jnp.float32, jnp.bfloat16


def dot(a, b):
    return jnp.dot(a, b, preferred_element_type=F32)


def split(a):
    hi = a.astype(BF16)
    return hi, (a - hi.astype(F32)).astype(BF16)


def stack(a):
    hi = a.astype(BF16).astype(F32)
    return jnp.concatenate([hi, a - hi], axis=0).astype(BF16)


def fold_rows(a):
    half = a.shape[0] // 2
    return a[:half] + a[half:]


def dot3(a, bh, bl):
    return fold_rows(dot(stack(a), bh)) + dot(a.astype(BF16), bl)


def iotas(shape):
    return (
        lax.broadcasted_iota(jnp.int32, shape, 0),
        lax.broadcasted_iota(jnp.int32, shape, 1),
    )


def div(x, n):
    return x >> (n.bit_length() - 1) if n & (n - 1) == 0 else lax.div(x, jnp.int32(n))


def rem(x, n):
    return x & (n - 1) if n & (n - 1) == 0 else lax.rem(x, jnp.int32(n))


def block_diagonal(w, copies):
    rows, cols = w.shape
    wide = jnp.concatenate([w] * copies, axis=1)
    tall = jnp.concatenate([wide] * copies, axis=0)
    r, c = iotas(tall.shape)
    return jnp.where(div(r, rows) == div(c, cols), tall, 0.0)


def kernel(n_row, n_col, heads, fold, columns, *refs):
    inputs, (a_out, upd_out), local = refs[:12], refs[12:14], refs[14:26]
    x_in, w_in, ag_ref, v_ref, g_ref, ot_ref, og_ref, lwt_ref, rwt_ref, bias_ref, ow, pair = local
    (
    x_ref, w_ref, xbuf, wbuf, lr, lbuf, rbuf, wp, perm, lp, th, tl,
    bd_v, bd_g, bd_o, bd_lr,
    sx, rx, sw, rws, sl, rl, sr, rr, in_sem,
    ) = refs[26:]
    r, c = lax.axis_index("row"), lax.axis_index("col")
    rows, width = x_ref.shape
    channels = v_ref.shape[0]
    seqs = width // channels
    factor = lwt_ref.shape[0]
    lanes = seqs * factor
    all_seqs = seqs * n_col
    per = columns // rows
    home = r // per
    slot = r % per
    is_home = home == c
    mine = (r, c)

    loads = [pltpu.make_async_copy(a, b, in_sem.at[k]) for k, (a, b) in enumerate(zip(inputs, local))]
    for load in loads:
        load.start()

    barrier = pltpu.get_barrier_semaphore()
    for k in range(1, n_row):
        pl.semaphore_signal(barrier, 1, device_id=((r + k) % n_row, c), device_id_type=MESH)
    for k in range(1, n_col):
        pl.semaphore_signal(barrier, 1, device_id=(r, (c + k) % n_col), device_id_type=MESH)
    for a in range(per):
        for k in range(n_col):
            src_r = c * per + a

            @pl.when(jnp.logical_and(src_r != r, k != c))
            def _():
                pl.semaphore_signal(barrier, 1, device_id=(src_r, jnp.int32(k)), device_id_type=MESH)

    loads[0].wait()
    loads[1].wait()
    x_ref[...] = jnp.concatenate([x_in[:, s, :] for s in range(seqs)], axis=1)
    half = w_ref.shape[0]
    packed = [w_in[a * half : (a + 1) * half, :] for a in range(fold)]
    kpad = w_ref.shape[1] - fold * columns
    if kpad:
        packed.append(jnp.zeros((half, kpad), F32))
    w_ref[...] = jnp.concatenate(packed, axis=1)

    @pl.when(is_home)
    def _():
        pl.semaphore_wait(barrier, n_row - 1 + n_col - 1)

    @pl.when(jnp.logical_not(is_home))
    def _():
        pl.semaphore_wait(barrier, n_row - 1 + n_col - 1 + n_row - 1)

    def remote(src, dst, send, recv, device):
        return pltpu.make_async_remote_copy(
            src_ref=src, dst_ref=dst, send_sem=send, recv_sem=recv,
            device_id=device, device_id_type=MESH,
        )

    sends = []
    for k in range(1, n_col):
        cp = remote(w_ref, wbuf.at[c], sw.at[k], rws.at[c], (r, (c + k) % n_col))
        cp.start()
        sends.append(cp)
    for k in range(1, n_row):
        cp = remote(x_ref, xbuf.at[r], sx.at[k], rx.at[r], ((r + k) % n_row, c))
        cp.start()
        sends.append(cp)

    xbuf[r] = x_ref[...]
    wbuf[c] = w_ref[...]
    for load in loads[2:-1]:
        load.wait()
    part = v_ref.shape[1] // fold
    o_w = ot_ref[...].T
    for a in range(fold):
        lo_l, hi_l = a * part, (a + 1) * part
        for ref, bd, w in (
            (v_ref, bd_v, v_ref[:, lo_l:hi_l]),
            (g_ref, bd_g, g_ref[:, lo_l:hi_l]),
            (ot_ref, bd_o, o_w[lo_l:hi_l, :]),
        ):
            h, l = split(block_diagonal(w, seqs))
            bd[a, 0] = h
            bd[a, 1] = l
    h, l = split(
        jnp.concatenate(
            [block_diagonal(ref[...].T, seqs) for ref in (lwt_ref, rwt_ref)], axis=1
        )
    )
    bd_lr[0] = h
    bd_lr[1] = l
    pr, pc = iotas(perm.shape)
    perm[...] = jnp.where(
        pr == rem(pc, all_seqs) * factor + div(pc, all_seqs), 1.0, 0.0
    ).astype(BF16)

    mr, mc = iotas((width, width))
    mean_of = jnp.where(div(mr, channels) == div(mc, channels), 1.0 / channels, 0.0).astype(BF16)

    def normalize(x, gain):
        cen = x - fold_rows(dot(stack(x), mean_of))
        var = fold_rows(dot(stack(cen * cen), mean_of))
        return cen * lax.rsqrt(var + 1e-05) * gain

    gain = jnp.concatenate([ag_ref[...]] * seqs, axis=1)
    out_gain = jnp.concatenate([og_ref[...]] * seqs, axis=1)
    own = normalize(x_ref[...], gain)
    gates = [
        1.0 / (1.0 + jnp.exp(-dot3(own, bd_g[a, 0], bd_g[a, 1]))) for a in range(fold)
    ]

    z = ow.shape[1]
    for d in range(factor):
        h, l = split(ow[pl.ds(d, factor, stride=factor), :])
        wp[:, d * z : (d + 1) * z] = jnp.concatenate([h, h, l], axis=0)

    for k in range(1, n_row):
        s = (r + k) % n_row
        remote(x_ref, xbuf.at[s], sx.at[k], rx.at[s], (s, c)).wait_recv()
    nh, nl = split(normalize(xbuf[...].reshape(n_row * rows, width), gain))

    def spread(n):
        parts = []
        for cc in range(n_col):
            blk = n[cc * columns : (cc + 1) * columns]
            for a in range(fold):
                parts.append(
                    jnp.concatenate(
                        [blk if b == a else jnp.zeros_like(blk) for b in range(fold)], axis=1
                    )
                )
            if kpad:
                parts.append(jnp.zeros((kpad, fold * width), BF16))
        return jnp.concatenate(parts, axis=0)

    sh, sl_ = spread(nh), spread(nl)
    for k in range(1, n_col):
        s = (c + k) % n_col
        remote(w_ref, wbuf.at[s], sw.at[k], rws.at[s], (r, s)).wait_recv()
    wide = jnp.concatenate([wbuf[cc] for cc in range(n_col)], axis=1)
    mixed = dot3(wide, sh, sl_)
    hpart = heads // fold
    head_dim = part // hpart
    res = x_ref[...]
    for a in range(fold):
        full = dot3(mixed[:, a * width : (a + 1) * width], bd_v[a, 0], bd_v[a, 1])
        _, lane = iotas((rows, seqs * part))
        head_of = rem(div(lane, head_dim), hpart)
        avg = jnp.zeros((rows, seqs * part), F32)
        for hh in range(hpart):
            avg = jnp.where(head_of == hh, full[hh * rows : (hh + 1) * rows], avg)
        res = res + dot3(gates[a] * avg, bd_o[a, 0], bd_o[a, 1])
    for s in range(seqs):
        a_out[:, s, :] = res[:, s * channels : (s + 1) * channels]
    both = dot3(normalize(res, out_gain), bd_lr[0], bd_lr[1])
    lr[0] = both[:, :lanes]
    lr[1] = both[:, lanes:]

    for k in range(1, n_col):
        cp = remote(lr.at[0], lbuf.at[c], sl.at[k], rl.at[c], (r, (c + k) % n_col))
        cp.start()
        sends.append(cp)
    for k in range(1, n_row):
        cp = remote(lr.at[1], rbuf.at[slot, c], sr.at[k], rr.at[slot, c], ((r + k) % n_row, home))
        cp.start()
        sends.append(cp)
    to_home = remote(lr.at[1], rbuf.at[slot, c], sr.at[0], rr.at[slot, c], (r, home))

    @pl.when(jnp.logical_not(is_home))
    def _():
        to_home.start()

    @pl.when(is_home)
    def _():
        rbuf[slot, c] = both[:, lanes:]

    lbuf[c] = both[:, :lanes]
    for k in range(1, n_col):
        s = (c + k) % n_col
        remote(lr.at[0], lbuf.at[s], sl.at[k], rl.at[s], (r, s)).wait_recv()
    for cc in range(n_col):
        blk = lbuf[cc]
        hi = blk.astype(BF16).astype(F32)
        lo = blk - hi
        for s in range(seqs):
            cut = slice(s * factor, (s + 1) * factor)
            pieces = [hi[:, cut], lo[:, cut], hi[:, cut], jnp.zeros((rows, lp.shape[1] - 3 * factor), F32)]
            lp[pl.ds(cc * seqs + s, rows, stride=all_seqs), :] = jnp.concatenate(pieces, axis=1)

    pairs = th.shape[0]
    block = pairs * 2

    def make_t(first):
        left = lp[pl.ds(pl.multiple_of(first * all_seqs, 8), block * all_seqs), :][
            :, : 3 * factor
        ].astype(BF16)
        for d in range(0, factor, 2):
            t = dot(left, wp[:, d * z : (d + 2) * z])
            for e in range(2):
                h, l = split(t[:, e * z : (e + 1) * z])
                h = h.reshape(pairs, 2, all_seqs, z)
                l = l.reshape(pairs, 2, all_seqs, z)
                at = slice((d + e) * all_seqs, (d + e + 1) * all_seqs)
                for q in range(2):
                    th[:, at, q * z : (q + 1) * z] = h[:, q]
                    tl[:, at, q * z : (q + 1) * z] = l[:, q]

    make_t(0)

    for a in range(per):
        for cc in range(n_col):

            @pl.when(jnp.logical_not(jnp.logical_and(c * per + a == r, cc == c)))
            def _():
                remote(
                    lr.at[1], rbuf.at[a, cc], sr.at[0], rr.at[a, cc], (c * per + a, jnp.int32(cc))
                ).wait_recv()

    right = jnp.concatenate(
        [jnp.concatenate([rbuf[a, cc] for cc in range(n_col)], axis=1) for a in range(per)], axis=0
    ) * (1.0 / all_seqs)
    right2 = dot(stack(right), perm[...]).astype(BF16)
    right1 = right2[:columns]

    bias2 = jnp.concatenate([bias_ref[...]] * 2, axis=1)

    def finish(first):
        for q in range(pairs):
            u = fold_rows(dot(right2, th[q])) + dot(right1, tl[q]) + bias2
            upd_out[first + 2 * q] = pair[first + 2 * q] + u[:, :z]
            upd_out[first + 2 * q + 1] = pair[first + 2 * q + 1] + u[:, z:]

    loads[-1].wait()
    finish(0)
    if rows > block:

        def step(i, _):
            make_t(i * block)
            finish(i * block)
            return 0

        lax.fori_loop(1, rows // block, step, 0)

    for cp in sends:
        cp.wait_send()

    @pl.when(jnp.logical_not(is_home))
    def _():
        to_home.wait_send()


def on_device(
    n_row, n_col,
    alignment, pair_state, pair_weights, align_gain, value_weight, gate_weight,
    output_weight, outer_gain, left_weight, right_weight, outer_weight, outer_bias,
):
    heads = pair_weights.shape[0]
    rows, seqs, channels = alignment.shape
    columns = pair_state.shape[1]
    z = pair_state.shape[2]
    factor = left_weight.shape[1]
    hidden = value_weight.shape[1]
    all_seqs = seqs * n_col
    width = seqs * channels
    fold = max(1, 128 // columns)
    while heads % fold:
        fold -= 1
    wide = -(-fold * columns // 128) * 128
    half = heads // fold * rows
    block = 2
    for b in range(2, rows + 1, 2):
        if rows % b == 0 and b * all_seqs <= 384:
            block = b
    per = columns // rows
    part = hidden // fold
    vmem = pl.BlockSpec(memory_space=pltpu.VMEM)
    dma = pltpu.SemaphoreType.DMA
    operands = (
        alignment, pair_weights.reshape(heads * rows, columns), align_gain.reshape(1, -1),
        value_weight, gate_weight, output_weight.T, outer_gain.reshape(1, -1),
        left_weight.T, right_weight.T, outer_bias.reshape(1, -1), outer_weight,
        pair_state,
    )
    return pl.pallas_call(
        functools.partial(kernel, n_row, n_col, heads, fold, columns),
        name="msa_block",
        out_shape=(
            pltpu.VMEM(alignment.shape, F32),
            pltpu.VMEM((rows, columns, z), F32),
        ),
        in_specs=[pl.BlockSpec(memory_space=pltpu.HBM)] * len(operands),
        out_specs=(vmem, vmem),
        scratch_shapes=[pltpu.VMEM(operand.shape, F32) for operand in operands]
        + [
            pltpu.VMEM((rows, width), F32),
            pltpu.VMEM((half, wide), F32),
            pltpu.VMEM((n_row, rows, width), F32),
            pltpu.VMEM((n_col, half, wide), F32),
            pltpu.VMEM((2, rows, seqs * factor), F32),
            pltpu.VMEM((n_col, rows, seqs * factor), F32),
            pltpu.VMEM((per, n_col, rows, seqs * factor), F32),
            pltpu.VMEM((3 * factor, factor * z), BF16),
            pltpu.VMEM((all_seqs * factor, all_seqs * factor), BF16),
            pltpu.VMEM((rows * all_seqs, 128), F32),
            pltpu.VMEM((block // 2, all_seqs * factor, 2 * z), BF16),
            pltpu.VMEM((block // 2, all_seqs * factor, 2 * z), BF16),
            pltpu.VMEM((fold, 2, width, seqs * part), BF16),
            pltpu.VMEM((fold, 2, width, seqs * part), BF16),
            pltpu.VMEM((fold, 2, seqs * part, width), BF16),
            pltpu.VMEM((2, width, 2 * seqs * factor), BF16),
            dma((n_row,)),
            dma((n_row,)),
            dma((n_col,)),
            dma((n_col,)),
            dma((n_col,)),
            dma((n_col,)),
            dma((n_row,)),
            dma((per, n_col)),
            dma((len(operands),)),
        ],
        compiler_params=pltpu.CompilerParams(collective_id=0, has_side_effects=True, vmem_limit_bytes=67043328 - 4 * rows * columns * z - (64 << 10)),
    )(*operands)


def solution(mesh):
    n_row, n_col = mesh.shape["row"], mesh.shape["col"]
    return jax.shard_map(
        functools.partial(on_device, n_row, n_col),
        mesh=mesh,
        in_specs=(
            P("row", "col", None),
            P("row", "col", None),
            P(None, "row", "col"),
        )
        + (P(),) * 9,
        out_specs=(P("row", "col", None), P("row", "col", None)),
        check_vma=False,
    )
```
